32 devices in a mesh: wide: 16 (over z, x, core), narrow: 2 (over y).
Axes of the slice: x: 2, y: 2, z: 4, core: 2. Of those that a mesh axis runs over, the one named last changes fastest.
Arguments:
- activations: bfloat16 [4096, 8192], P('narrow', 'wide'), may hold values from -6 to 6
- cotangent: bfloat16 [4096, 4096], P('wide', 'narrow'), may hold values from -6 to 6
- sign_bits: int32 [8192, 4096], P('wide', 'narrow'), may hold values from 0 to 1
- seg_lengths: int32 [4], replicated, may hold values from 1 to 1536, 4096 in all
- kept_index: int32 [16384], replicated, may hold values from 0 to 33554431
Outputs:
- sketch: float32 [4, 16384], P(None, ('wide', 'narrow'))
The draws below stay inside these ranges and needn't reach their ends.
Inputs may be any that keep to these rules, and one draw needn't show every extreme that they name: `seg_lengths`: the lengths sum to 4096; the longest is exactly 1536.
All inputs are finite; a program needn't handle non-finite values.
Results may differ from the reference program's by a relative error of at most 0.0003.
Values may be sent and summed in bfloat16 or wider, within the bound.
A program may use at most 192 MiB of HBM per device.

```python
import math
import jax
import jax.numpy as jnp
import numpy as np
from jax import lax

D = 8192
H = 4096
KEEP = 16384
SEG = 4
MOST = 1536
TOKENS = 4096
N_WIDE = 16
N_NARROW = 2


def with_ends(entries, stream_key, smallest, top_value):
    longest = entries.shape.index(max(entries.shape))
    spots = []
    for shift in (0, 1):
        where = [jax.random.randint(jax.random.fold_in(stream_key, axis), (), 0, length) for axis, length in enumerate(entries.shape)]
        where[longest] = (where[longest] + shift) % entries.shape[longest]
        spots.append(tuple(where))
    return entries.at[spots[0]].set(smallest).at[spots[1]].set(top_value)


def shard_levels(rng, shape, split, smallest, high):
    gain = 1.0
    for axis_at, blocks in split:
        steps = jax.random.uniform(jax.random.fold_in(jax.random.fold_in(rng, 6), axis_at), (blocks,), jnp.float32, smallest / len(split), high / len(split))
        gain = gain * jnp.repeat(jnp.exp(steps), shape[axis_at] // blocks).reshape((-1,) + (1,) * (len(shape) - 1 - axis_at))
    return gain


def length_profile(number_of, total, reach, slope):
    weights = [(1 << 20) // math.isqrt(grade ** slope) + 1 for grade in range(2, number_of + 1)]
    rest, counts = total - reach - (number_of - 1), [1] * (number_of - 1)
    while rest > 0:
        movable = [i for i in range(number_of - 1) if counts[i] < reach]
        whole, remaining = sum([weights[i] for i in movable]), rest
        for i in movable:
            extra = min(reach - counts[i], max(1, remaining * weights[i] // whole), rest)
            counts[i] = counts[i] + extra
            rest = rest - extra
    return np.array([reach] + counts)


def ragged_sizes(stream_key, amount, total, most, skew):
    if amount == 2:
        one = jax.random.randint(stream_key, (), max(1, total - most), min(most, total - 1) + 1)
        return jnp.stack([one, total - one])
    lengths = jnp.asarray(length_profile(amount, total, most, skew), jnp.int32)
    couples = (amount - 1) // 2
    donor, sink = lengths[1:1 + 2 * couples:2], lengths[2:2 + 2 * couples:2]
    room = jnp.minimum(donor - 1, most - sink)
    passed = jax.random.randint(jax.random.fold_in(stream_key, 1), (couples,), 0, 1 << 20) % (room + 1)
    lengths = lengths.at[1:1 + 2 * couples:2].set(donor - passed).at[2:2 + 2 * couples:2].set(sink + passed)
    return lengths[jax.random.permutation(jax.random.fold_in(stream_key, 2), amount)]


def scatter_about(key, shape, width, bound, split=(), kind=jnp.bfloat16):
    gain = shard_levels(key, shape, split, -0.22, 0.18) if split else 1.0
    values = jax.random.normal(key, shape, jnp.float32) * width * gain
    return jnp.minimum(jnp.maximum(values, -bound), bound).astype(kind)


def setup_inputs(seed: int = 0) -> dict:
    streams_of = jax.random.split(jax.random.key(seed), 6)
    return {
        "activations": scatter_about(streams_of[0], (TOKENS, D), 1.0, 6.0, ((0, 2), (1, 16))),
        "cotangent": scatter_about(streams_of[1], (TOKENS, H), 1.0, 6.0, ((0, 16), (1, 2))),
        "sign_bits": with_ends(jax.random.randint(streams_of[2], (D, H), 0, 2), jax.random.fold_in(streams_of[2], 1), 0, 1).astype(jnp.int32),
        "seg_lengths": ragged_sizes(streams_of[3], SEG, TOKENS, MOST, 1).astype(jnp.int32),
        "kept_index": with_ends(jax.random.randint(streams_of[4], (KEEP,), 0, D * H), jax.random.fold_in(streams_of[4], 1), 0, (D * H) - 1).astype(jnp.int32),
    }


def sylvester(extent):
    indices = jnp.arange(extent, dtype=jnp.int32)
    common = indices[:, None] & indices[None, :]
    parity = jnp.zeros((extent, extent), jnp.int32)
    for bit_pos in range(extent.bit_length() - 1):
        parity = parity + (common >> bit_pos & 1)
    return (1 - 2 * (parity % 2)).astype(jnp.float32)

def reference(activations, cotangent, sign_bits, seg_lengths, kept_index):
    highest = lax.Precision.HIGHEST
    total_tok = activations.shape[0]
    starts = (jnp.cumsum(seg_lengths) - seg_lengths).astype(jnp.int32)
    signs = (1 - 2 * sign_bits).astype(jnp.float32)
    rows_local = D // N_WIDE
    cols_local = H // N_NARROW
    left_local = sylvester(rows_local)
    left_outer = sylvester(N_WIDE)
    right_local = sylvester(cols_local)
    right_outer = sylvester(N_NARROW)
    scale = 1.0 / math.sqrt(D * H)

    def one_segment(packed):
        begin_at, count = packed
        clamped = jnp.minimum(begin_at, total_tok - MOST).astype(jnp.int32)
        rows_x = lax.dynamic_slice_in_dim(activations, clamped, MOST, 0).astype(jnp.float32)
        rows_c = lax.dynamic_slice_in_dim(cotangent, clamped, MOST, 0).astype(jnp.float32)
        where_at = clamped + jnp.arange(MOST, dtype=jnp.int32)
        inside = (where_at >= begin_at) & (where_at < begin_at + count)
        rows_c = jnp.where(inside[:, None], rows_c, jnp.zeros((), jnp.float32))
        grad = jnp.dot(rows_x.T, rows_c, precision=highest)
        signed = grad * lax.rsqrt(count.astype(jnp.float32)) * signs
        blocks = signed.reshape(N_WIDE, rows_local, H)
        blocks = jnp.einsum('ab,wbh->wah', left_local, blocks, precision=highest)
        blocks = jnp.einsum('vw,wah->vah', left_outer, blocks, precision=highest)
        blocks = blocks.reshape(D, N_NARROW, cols_local)
        blocks = jnp.einsum('dnc,ce->dne', blocks, right_local, precision=highest)
        blocks = jnp.einsum('dne,nm->dme', blocks, right_outer, precision=highest)
        return jnp.take(blocks.reshape(-1), kept_index) * scale
    return lax.map(one_segment, (starts, seg_lengths))
```

```python
import functools
import math

import jax
import jax.numpy as jnp
import numpy as np
from jax import lax
from jax.experimental import pallas as pl
from jax.experimental.pallas import tpu as pltpu
from jax.sharding import PartitionSpec as P

LANES = 128
MESH = pl.DeviceIdType.MESH


def sylvester(extent):
    indices = np.arange(extent)
    common = indices[:, None] & indices[None, :]
    parity = np.zeros((extent, extent), np.int64)
    for bit_pos in range(extent.bit_length() - 1):
        parity += common >> bit_pos & 1
    return jnp.asarray(1 - 2 * (parity % 2), jnp.bfloat16)


def spread_kernel(
    n_wide, n_narrow, cross,
    acts, cots, acts_all, cots_all,
    acts_own, cots_own, local_sem, acts_send, acts_recv, cots_send, cots_recv,
):
    wide = lax.axis_index("wide")
    narrow = lax.axis_index("narrow")
    lines = n_wide // (2 * cross)
    core = lax.rem(wide, 2)
    side = lax.rem(wide // 2, cross)
    place = wide // (2 * cross)
    tok_acts = acts.shape[0]
    tok_cots = cots.shape[0]

    def index_of(at, across, on_core):
        return (at * cross + across) * 2 + on_core

    partner = index_of(place, side, 1 - core)
    up = index_of(lax.rem(place + 1, lines), side, core)
    down = index_of(lax.rem(place + lines - 1, lines), side, core)
    across = [lax.rem(side + off, cross) for off in range(1, cross)]
    has_up = place < lines - 1
    has_down = place > 0

    barrier = pltpu.get_barrier_semaphore()

    def greet(**where):
        pl.semaphore_signal(barrier, inc=1, device_id=where, device_id_type=MESH)

    greet(wide=partner)
    for other in across:
        greet(wide=index_of(place, other, core))
    for off in range(1, n_narrow):
        greet(narrow=lax.rem(narrow + off, n_narrow))

    @pl.when(has_up)
    def _():
        greet(wide=up)

    @pl.when(has_down)
    def _():
        greet(wide=down)

    ends = jnp.where(has_up, 1, 0) + jnp.where(has_down, 1, 0)
    pl.semaphore_wait(barrier, 1 + (cross - 1) + (n_narrow - 1) + ends)

    def acts_copy(off):
        return pltpu.make_async_remote_copy(
            src_ref=acts,
            dst_ref=acts_all.at[pl.ds(narrow * tok_acts, tok_acts), :],
            send_sem=acts_send.at[off],
            recv_sem=acts_recv.at[off],
            device_id={"narrow": lax.rem(narrow + off, n_narrow)},
            device_id_type=MESH,
        )

    def cots_copy(way, shard, to, own):
        window = pl.ds(shard * tok_cots, tok_cots)
        return pltpu.make_async_remote_copy(
            src_ref=cots if own else cots_all.at[window, :],
            dst_ref=cots_all.at[window, :],
            send_sem=cots_send.at[way, shard],
            recv_sem=cots_recv.at[shard],
            device_id={"wide": to},
            device_id_type=MESH,
        )

    def outgoing(shard, own, climbs, drops, crosses):
        todo = []
        if climbs:
            todo.append((has_up, cots_copy(0, shard, up, own)))
        if drops:
            todo.append((has_down, cots_copy(1, shard, down, own)))
        if crosses:
            for at, other in enumerate(across):
                to = index_of(place, other, core)
                todo.append((None, cots_copy(3 + at, shard, to, own)))
        todo.append((None, cots_copy(2, shard, partner, own)))
        return todo

    def each(todo, act):
        for condition, copy in todo:
            if condition is None:
                act(copy)
            else:
                pl.when(condition)(functools.partial(act, copy))

    def start(copy):
        copy.start()

    def sent(copy):
        copy.wait_send()

    def arrived(shard):
        cots_copy(2, shard, partner, False).wait_recv()

    mine = outgoing(wide, True, True, True, True)
    each(mine, start)
    for off in range(1, n_narrow):
        acts_copy(off).start()

    to_vmem = (
        pltpu.make_async_copy(acts, acts_own, local_sem.at[0]),
        pltpu.make_async_copy(cots, cots_own, local_sem.at[1]),
    )
    from_vmem = (
        pltpu.make_async_copy(
            acts_own, acts_all.at[pl.ds(narrow * tok_acts, tok_acts), :], local_sem.at[2]
        ),
        pltpu.make_async_copy(
            cots_own, cots_all.at[pl.ds(wide * tok_cots, tok_cots), :], local_sem.at[3]
        ),
    )
    for copy in to_vmem:
        copy.start()
    for copy, back in zip(to_vmem, from_vmem):
        copy.wait()
        back.start()

    def below(step):
        return place - step >= 0, index_of(place - step, side, core)

    def above(step):
        return place + step < lines, index_of(place + step, side, core)

    def crossed(step):
        for other in across:
            if step == 0:
                shard = index_of(place, other, core)
                arrived(shard)
                each(outgoing(shard, False, False, False, False), start)
                continue

            @pl.when(place - step >= 0)
            def _():
                shard = index_of(place - step, other, core)
                arrived(shard)
                each(outgoing(shard, False, False, False, False), start)

            @pl.when(place + step < lines)
            def _():
                shard = index_of(place + step, other, core)
                arrived(shard)
                each(outgoing(shard, False, False, False, False), start)

    for step in range(1, lines):
        there, shard_below = below(step)

        @pl.when(there)
        def _():
            arrived(shard_below)
            each(outgoing(shard_below, False, True, False, True), start)

        there, shard_above = above(step)

        @pl.when(there)
        def _():
            arrived(shard_above)
            each(outgoing(shard_above, False, False, True, True), start)

        crossed(step - 1)
    crossed(lines - 1)

    for at in range(lines):
        for over in range(cross):
            arrived(index_of(at, over, 1 - core))
    for off in range(1, n_narrow):
        acts_copy(off).wait()
    for copy in from_vmem:
        copy.wait()
    each(mine, sent)
    for step in range(1, lines):
        there, shard_below = below(step)

        @pl.when(there)
        def _():
            each(outgoing(shard_below, False, True, False, True), sent)

        there, shard_above = above(step)

        @pl.when(there)
        def _():
            each(outgoing(shard_above, False, False, True, True), sent)

    for at in range(lines):
        for other in across:
            shard = index_of(at, other, core)
            each(outgoing(shard, False, False, False, False), sent)


def spread(acts, cots, n_wide, n_narrow):
    cross = 2
    anywhere = pl.BlockSpec(memory_space=pl.ANY)
    return pl.pallas_call(
        functools.partial(spread_kernel, n_wide, n_narrow, cross),
        out_shape=(
            jax.ShapeDtypeStruct((acts.shape[0] * n_narrow, acts.shape[1]), acts.dtype),
            jax.ShapeDtypeStruct((cots.shape[0] * n_wide, cots.shape[1]), cots.dtype),
        ),
        in_specs=[anywhere, anywhere],
        out_specs=(anywhere, anywhere),
        scratch_shapes=[
            pltpu.VMEM(acts.shape, acts.dtype),
            pltpu.VMEM(cots.shape, cots.dtype),
            pltpu.SemaphoreType.DMA((4,)),
            pltpu.SemaphoreType.DMA((n_narrow,)),
            pltpu.SemaphoreType.DMA((n_narrow,)),
            pltpu.SemaphoreType.DMA((2 + cross, n_wide)),
            pltpu.SemaphoreType.DMA((n_wide,)),
        ],
        compiler_params=pltpu.CompilerParams(collective_id=0, has_side_effects=True),
        name="spread",
    )(acts, cots)


def butterflies(parts):
    parts = list(parts)
    gap = 1
    while gap < len(parts):
        for low in range(len(parts)):
            if not low & gap:
                one, two = parts[low], parts[low | gap]
                parts[low], parts[low | gap] = one + two, one - two
        gap *= 2
    return parts


def halves(values):
    high = values.astype(jnp.bfloat16)
    low = (values - high.astype(jnp.float32)).astype(jnp.bfloat16)
    return high, low


def sketch_kernel(
    seg_count, steps_ref, spots_ref, gains_ref,
    acts_ref, cots_ref, bits_ref, left_ref, right_ref, signs_ref,
    out_ref, flipped, total, table,
):
    step = pl.program_id(0)
    tile = steps_ref[0, step]
    seg = steps_ref[1, step]
    first = steps_ref[2, step]
    last = steps_ref[3, step]
    low = steps_ref[4, step]
    high = steps_ref[5, step]
    tok = acts_ref.shape[0]
    rows, cols = bits_ref.shape
    row_block = left_ref.shape[0]
    col_block = right_ref.shape[0]
    row_groups = rows // row_block
    col_groups = cols // col_block

    @pl.when(low < high)
    def _():
        where_at = tile * tok + lax.broadcasted_iota(jnp.int32, acts_ref.shape, 0)
        inside = (where_at >= low) & (where_at < high)
        values = jnp.where(inside, acts_ref[...].astype(jnp.float32), 0.0)
        flipped[...] = values.T.astype(jnp.bfloat16)

        def columns(at, _):
            window = pl.ds(pl.multiple_of(at * col_block, col_block), col_block)
            grad = jnp.dot(
                flipped[...], cots_ref[:, window], preferred_element_type=jnp.float32
            )

            @pl.when(first == 1)
            def _():
                total[:, window] = grad

            @pl.when(first == 0)
            def _():
                total[:, window] += grad

            return 0

        lax.fori_loop(0, col_groups, columns, 0)

    @pl.when(last == 1)
    def _():
        gain = gains_ref[seg]

        def columns(at, _):
            window = pl.ds(pl.multiple_of(at * col_block, col_block), col_block)
            parts = []
            for group in range(row_groups):
                part = pl.ds(group * row_block, row_block)
                sign = (1 - 2 * bits_ref[part, window]).astype(jnp.float32)
                parts.append(total[part, window] * (sign * gain))
            for group, part in enumerate(butterflies(parts)):
                upper, lower = halves(part)
                mixed = jnp.dot(
                    left_ref[...], upper, preferred_element_type=jnp.float32
                ) + jnp.dot(left_ref[...], lower, preferred_element_type=jnp.float32)
                upper, lower = halves(mixed)
                mixed = jnp.dot(
                    upper, right_ref[...], preferred_element_type=jnp.float32
                ) + jnp.dot(lower, right_ref[...], preferred_element_type=jnp.float32)
                total[pl.ds(group * row_block, row_block), window] = mixed
            return 0

        lax.fori_loop(0, col_groups, columns, 0)
        per_group = col_block // LANES

        def across(at, _):
            base = pl.multiple_of(at * 8, 8)
            for lane_block in range(per_group):
                parts = [
                    total[pl.ds(base, 8), pl.ds(group * col_block + lane_block * LANES, LANES)]
                    for group in range(col_groups)
                ]
                for group, part in enumerate(butterflies(parts)):
                    block = group * per_group + lane_block
                    begin = (block * rows + base) * seg_count + seg
                    table[pl.ds(begin, 8, stride=seg_count), :] = part
            return 0

        lax.fori_loop(0, rows // 8, across, 0)

    @pl.when(step == pl.num_programs(0) - 1)
    def _():
        lane = lax.broadcasted_iota(jnp.int32, (8, LANES), 1)
        chains = 4

        def pick(group, _):
            found = [jnp.zeros((8, LANES), jnp.float32)] * chains
            for at in range(LANES):
                spot = spots_ref[group * LANES + at]
                values = table[pl.ds(lax.shift_right_logical(spot, 7), 8), :]
                values = pltpu.roll(values, spot & (LANES - 1), 1)
                found[at % chains] = jnp.where(lane == at, values, found[at % chains])
            both = (found[0] + found[1]) + (found[2] + found[3])
            out_ref[group] = both[:seg_count] * signs_ref[pl.ds(group, 1), :]
            return 0

        lax.fori_loop(0, out_ref.shape[0], pick, 0)


def local_sketch(acts, cots, bits, lengths, spots, signs):
    tokens = acts.shape[0]
    rows, cols = bits.shape
    seg_count = lengths.shape[0]
    groups = signs.shape[0]
    tok = 256
    row_block, col_block = min(rows, 256), min(cols, 256)
    steps = tokens // tok + seg_count - 1
    ends = jnp.cumsum(lengths)
    starts = ends - lengths
    first_tile = starts // tok
    tiles = (ends + tok - 1) // tok - first_tile
    after = jnp.cumsum(tiles)
    before = after - tiles
    at = jnp.arange(steps, dtype=jnp.int32)
    seg = jnp.sum((at[:, None] >= after[None, :-1]).astype(jnp.int32), axis=1)
    mine = (seg[:, None] == jnp.arange(seg_count)[None, :]).astype(jnp.int32)

    def of(values):
        return jnp.sum(mine * values[None, :], axis=1)

    begun = of(before)
    tile = jnp.minimum(of(first_tile) + at - begun, tokens // tok - 1)
    live = at < after[-1]
    low = jnp.where(live, of(starts), 0)
    high = jnp.where(live, of(ends), 0)
    table = jnp.stack(
        [
            tile,
            seg,
            (at == begun).astype(jnp.int32),
            (at == of(after) - 1).astype(jnp.int32),
            low,
            high,
        ]
    ).astype(jnp.int32)
    gains = lax.rsqrt(lengths.astype(jnp.float32))
    fixed = lambda i, *_: (0, 0)
    return pl.pallas_call(
        functools.partial(sketch_kernel, seg_count),
        out_shape=jax.ShapeDtypeStruct((groups, seg_count, LANES), jnp.float32),
        grid_spec=pltpu.PrefetchScalarGridSpec(
            num_scalar_prefetch=3,
            grid=(steps,),
            in_specs=[
                pl.BlockSpec((tok, rows), lambda i, t, *_: (t[0, i], 0)),
                pl.BlockSpec((tok, cols), lambda i, t, *_: (t[0, i], 0)),
                pl.BlockSpec((rows, cols), fixed),
                pl.BlockSpec((row_block, row_block), fixed),
                pl.BlockSpec((col_block, col_block), fixed),
                pl.BlockSpec(signs.shape, fixed),
            ],
            out_specs=pl.BlockSpec((groups, seg_count, LANES), lambda i, *_: (0, 0, 0)),
            scratch_shapes=[
                pltpu.VMEM((rows, tok), jnp.bfloat16),
                pltpu.VMEM((rows, cols), jnp.float32),
                pltpu.VMEM((rows * cols // LANES * seg_count + 8, LANES), jnp.float32),
            ],
        ),
        compiler_params=pltpu.CompilerParams(vmem_limit_bytes=60 * 1024 * 1024),
        name="local_sketch",
    )(table, spots, gains, acts, cots, bits, sylvester(row_block), sylvester(col_block), signs)


def add_up_kernel(n_wide, n_narrow, shares, out, held, send_sem, recv_sem):
    count = n_wide * n_narrow
    me = lax.axis_index("wide") * n_narrow + lax.axis_index("narrow")
    barrier = pltpu.get_barrier_semaphore()

    def address(who):
        return {"wide": who // n_narrow, "narrow": lax.rem(who, n_narrow)}

    def greet(off, _):
        who = lax.rem(me + off, count)
        pl.semaphore_signal(barrier, inc=1, device_id=address(who), device_id_type=MESH)
        return 0

    lax.fori_loop(1, count, greet, 0)
    pl.semaphore_wait(barrier, count - 1)

    def copy_to(who, slot):
        return pltpu.make_async_remote_copy(
            src_ref=shares.at[who],
            dst_ref=held.at[slot],
            send_sem=send_sem.at[who],
            recv_sem=recv_sem.at[slot],
            device_id=address(who),
            device_id_type=MESH,
        )

    def send(off, _):
        copy_to(lax.rem(me + off, count), me).start()
        return 0

    lax.fori_loop(1, count, send, 0)
    out[...] = shares[me]

    def take(off, _):
        who = lax.rem(me + count - off, count)
        copy_to(who, who).wait_recv()
        out[...] += held[who]
        return 0

    lax.fori_loop(1, count, take, 0)

    def sent(off, _):
        copy_to(lax.rem(me + off, count), me).wait_send()
        return 0

    lax.fori_loop(1, count, sent, 0)


def add_up(shares, n_wide, n_narrow):
    count = n_wide * n_narrow
    in_vmem = pl.BlockSpec(memory_space=pltpu.VMEM)
    return pl.pallas_call(
        functools.partial(add_up_kernel, n_wide, n_narrow),
        out_shape=jax.ShapeDtypeStruct(shares.shape[1:], shares.dtype),
        in_specs=[in_vmem],
        out_specs=in_vmem,
        scratch_shapes=[
            pltpu.VMEM(shares.shape, shares.dtype),
            pltpu.SemaphoreType.DMA((count,)),
            pltpu.SemaphoreType.DMA((count,)),
        ],
        compiler_params=pltpu.CompilerParams(collective_id=1, has_side_effects=True),
        name="add_up",
    )(shares)


def body(n_wide, n_narrow, activations, cotangent, sign_bits, seg_lengths, kept_index):
    rows, cols = sign_bits.shape
    seg_count = seg_lengths.shape[0]
    kept = kept_index.shape[0]
    count = n_wide * n_narrow
    all_acts, all_cots = spread(activations, cotangent, n_wide, n_narrow)

    scale = 1.0 / math.sqrt(rows * n_wide * cols * n_narrow)
    full_cols = cols * n_narrow
    row_of = kept_index // full_cols
    col_of = kept_index % full_cols
    common = lax.population_count((row_of // rows) & lax.axis_index("wide"))
    common = common + lax.population_count((col_of // cols) & lax.axis_index("narrow"))
    signs = (1 - 2 * (common & 1)).astype(jnp.float32) * scale
    col = col_of % cols
    row = ((col // LANES) * rows + row_of % rows) * seg_count
    lane = jnp.arange(kept, dtype=jnp.int32)
    spots = row * LANES + ((lane - col) & (LANES - 1))
    shares = local_sketch(
        all_acts, all_cots, sign_bits, seg_lengths, spots, signs.reshape(-1, LANES)
    )
    each = kept // count
    if each % LANES:
        flat = shares.transpose(1, 0, 2).reshape(seg_count, kept)
        return lax.psum_scatter(flat, ("wide", "narrow"), scatter_dimension=1, tiled=True)
    mine = add_up(shares.reshape(count, -1, LANES), n_wide, n_narrow)
    mine = mine.reshape(each // LANES, seg_count, LANES)
    return mine.transpose(1, 0, 2).reshape(seg_count, each)


def solution(mesh):
    return jax.shard_map(
        functools.partial(body, mesh.shape["wide"], mesh.shape["narrow"]),
        mesh=mesh,
        in_specs=(P("narrow", "wide"), P("wide", "narrow"), P("wide", "narrow"), P(), P()),
        out_specs=P(None, ("wide", "narrow")),
        check_vma=False,
    )
```

```python
import functools
import math

import jax
import jax.numpy as jnp
import numpy as np
from jax import lax
from jax.experimental import pallas as pl
from jax.experimental.pallas import tpu as pltpu
from jax.sharding import PartitionSpec as P

LANES = 128
MOST = 1536
MESH = pl.DeviceIdType.MESH


def sylvester(extent):
    indices = np.arange(extent)
    common = indices[:, None] & indices[None, :]
    parity = np.zeros((extent, extent), np.int64)
    for bit_pos in range(extent.bit_length() - 1):
        parity += common >> bit_pos & 1
    return jnp.asarray(1 - 2 * (parity % 2), jnp.bfloat16)


def butterflies(parts):
    parts = list(parts)
    gap = 1
    while gap < len(parts):
        for low in range(len(parts)):
            if not low & gap:
                one, two = parts[low], parts[low | gap]
                parts[low], parts[low | gap] = one + two, one - two
        gap *= 2
    return parts


def halves(values):
    high = values.astype(jnp.bfloat16)
    low = (values - high.astype(jnp.float32)).astype(jnp.bfloat16)
    return high, low


def sketch_kernel(
    n_wide, n_narrow, cross, windows, n_chunks,
    bounds, gains, acts, cots, bits_in, left_ref, right_ref,
    out_ref, acts_all, bits_ref, flipped, table, bufs,
    local_sem, acts_send, acts_recv, cots_send, cots_recv,
):
    wide = lax.axis_index("wide")
    narrow = lax.axis_index("narrow")
    lines = n_wide // (2 * cross)
    core = lax.rem(wide, 2)
    side = lax.rem(wide // 2, cross)
    place = wide // (2 * cross)
    tok_acts = acts.shape[0]
    tok_cots = cots.shape[0]
    rows, cols = bits_in.shape
    row_block = left_ref.shape[0]
    col_block = right_ref.shape[0]
    row_groups = rows // row_block
    per_group = col_block // LANES
    seg_count = len(windows)
    stretch = per_group * rows * seg_count

    def index_of(at, across, on_core):
        return (at * cross + across) * 2 + on_core

    partner = index_of(place, side, 1 - core)
    up = index_of(lax.rem(place + 1, lines), side, core)
    down = index_of(lax.rem(place + lines - 1, lines), side, core)
    across = [lax.rem(side + off, cross) for off in range(1, cross)]
    has_up = place < lines - 1
    has_down = place > 0

    my_acts = pl.ds(narrow * tok_acts, tok_acts)
    my_cots = pl.ds(wide * tok_cots, tok_cots)

    def columns_of(chunk):
        return pl.ds(pl.multiple_of(chunk * col_block, col_block), col_block)

    def own_cots(chunk):
        return pltpu.make_async_copy(
            cots.at[:, columns_of(chunk)], bufs.at[chunk, my_cots, :], local_sem.at[2 + chunk]
        )

    def put_out(chunk):
        span = pl.ds(pl.multiple_of(chunk * stretch, 8), stretch)
        return pltpu.make_async_copy(
            table.at[span, :], out_ref.at[span, :], local_sem.at[2 + n_chunks + chunk]
        )

    own_acts = pltpu.make_async_copy(acts, acts_all.at[my_acts, :], local_sem.at[0])
    own_bits = pltpu.make_async_copy(bits_in, bits_ref, local_sem.at[1])
    for chunk in range(n_chunks):
        own_cots(chunk).start()
    own_acts.start()
    own_bits.start()

    barrier = pltpu.get_barrier_semaphore()

    def greet(**where):
        pl.semaphore_signal(barrier, inc=1, device_id=where, device_id_type=MESH)

    greet(wide=partner)
    for other in across:
        greet(wide=index_of(place, other, core))
    for off in range(1, n_narrow):
        greet(narrow=lax.rem(narrow + off, n_narrow))

    @pl.when(has_up)
    def _():
        greet(wide=up)

    @pl.when(has_down)
    def _():
        greet(wide=down)

    ends = jnp.where(has_up, 1, 0) + jnp.where(has_down, 1, 0)
    pl.semaphore_wait(barrier, 1 + (cross - 1) + (n_narrow - 1) + ends)

    def acts_copy(off):
        return pltpu.make_async_remote_copy(
            src_ref=acts,
            dst_ref=acts_all.at[my_acts, :],
            send_sem=acts_send.at[off],
            recv_sem=acts_recv.at[off],
            device_id={"narrow": lax.rem(narrow + off, n_narrow)},
            device_id_type=MESH,
        )

    def cots_copy(chunk, way, shard, to):
        place_of = bufs.at[chunk, pl.ds(shard * tok_cots, tok_cots), :]
        return pltpu.make_async_remote_copy(
            src_ref=place_of,
            dst_ref=place_of,
            send_sem=cots_send.at[way, chunk, shard],
            recv_sem=cots_recv.at[chunk, shard],
            device_id={"wide": to},
            device_id_type=MESH,
        )

    def outgoing(chunk, shard, climbs, drops, crosses):
        todo = []
        if climbs:
            todo.append((has_up, cots_copy(chunk, 0, shard, up)))
        if drops:
            todo.append((has_down, cots_copy(chunk, 1, shard, down)))
        if crosses:
            for at, other in enumerate(across):
                to = index_of(place, other, core)
                todo.append((None, cots_copy(chunk, 3 + at, shard, to)))
        todo.append((None, cots_copy(chunk, 2, shard, partner)))
        return todo

    def each(todo, act):
        for condition, copy in todo:
            if condition is None:
                act(copy)
            else:
                pl.when(condition)(functools.partial(act, copy))

    def start(copy):
        copy.start()

    def sent(copy):
        copy.wait_send()

    def arrived(chunk, shard):
        cots_copy(chunk, 2, shard, partner).wait_recv()

    def from_lines(chunk, step, act, wait):
        @pl.when(place - step >= 0)
        def _():
            shard = index_of(place - step, side, core)
            if wait:
                arrived(chunk, shard)
            each(outgoing(chunk, shard, True, False, True), act)

        @pl.when(place + step < lines)
        def _():
            shard = index_of(place + step, side, core)
            if wait:
                arrived(chunk, shard)
            each(outgoing(chunk, shard, False, True, True), act)

    def from_cross(chunk, step):
        for other in across:
            for sign in (1,) if step == 0 else (-1, 1):
                at = place + sign * step

                @pl.when((at >= 0) & (at < lines))
                def _():
                    shard = index_of(at, other, core)
                    arrived(chunk, shard)
                    each(outgoing(chunk, shard, False, False, False), start)

    def launch(chunk):
        own_cots(chunk).wait()
        each(outgoing(chunk, wide, True, True, True), start)

    def prepare():
        own_acts.wait()
        for off in range(1, n_narrow):
            acts_copy(off).wait()
        own_bits.wait()
        tile = 256
        offset = 0
        for seg, (low, high) in enumerate(windows):

            def one(at, _):
                begin = pl.multiple_of(low + at * tile, tile)
                values = acts_all[pl.ds(begin, tile), :].astype(jnp.float32)
                where_at = begin + lax.broadcasted_iota(jnp.int32, values.shape, 0)
                inside = (where_at >= bounds[0, seg]) & (where_at < bounds[1, seg])
                values = jnp.where(inside, values, 0.0)
                spot = pl.multiple_of(offset + at * tile, tile)
                flipped[:, pl.ds(spot, tile)] = values.T.astype(jnp.bfloat16)
                return 0

            lax.fori_loop(0, (high - low) // tile, one, 0)
            offset += high - low

    def compute(chunk):
        for at in range(lines):
            for over in range(cross):
                arrived(chunk, index_of(at, over, 1 - core))

        columns = columns_of(chunk)
        offset = 0
        for seg, (low, high) in enumerate(windows):
            grad = jnp.dot(
                flipped[:, offset : offset + high - low],
                bufs[chunk, low:high, :],
                preferred_element_type=jnp.float32,
            )
            offset += high - low
            sign = (1 - 2 * bits_ref[:, columns]).astype(jnp.float32)
            grad = grad * (sign * gains[seg])
            parts = [
                grad[group * row_block : (group + 1) * row_block]
                for group in range(row_groups)
            ]
            for group, part in enumerate(butterflies(parts)):
                upper, lower = halves(part)
                mixed = jnp.dot(
                    left_ref[...], upper, preferred_element_type=jnp.float32
                ) + jnp.dot(left_ref[...], lower, preferred_element_type=jnp.float32)
                upper, lower = halves(mixed)
                mixed = jnp.dot(
                    upper, right_ref[...], preferred_element_type=jnp.float32
                ) + jnp.dot(lower, right_ref[...], preferred_element_type=jnp.float32)
                for lane_block in range(per_group):
                    block = chunk * per_group + lane_block
                    base = (block * rows + group * row_block) * seg_count + seg
                    table[pl.ds(base, row_block, stride=seg_count), :] = mixed[
                        :, lane_block * LANES : (lane_block + 1) * LANES
                    ]
        put_out(chunk).start()

    launch(0)
    for off in range(1, n_narrow):
        acts_copy(off).start()

    def slot_work(slot, _):
        @pl.when(slot + 1 < n_chunks)
        def _():
            launch(slot + 1)

        for step in range(lines, 0, -1):
            chunk = slot + 1 - step

            @pl.when((chunk >= 0) & (chunk < n_chunks))
            def _():
                if step < lines:
                    from_lines(chunk, step, start, True)
                from_cross(chunk, step - 1)

        pl.when(slot == lines)(prepare)

        @pl.when(slot >= lines)
        def _():
            compute(slot - lines)

        return 0

    lax.fori_loop(0, n_chunks + lines, slot_work, 0)

    def finish(chunk, _):
        each(outgoing(chunk, wide, True, True, True), sent)
        for step in range(1, lines):
            from_lines(chunk, step, sent, False)
        for at in range(lines):
            for other in across:
                shard = index_of(at, other, core)
                each(outgoing(chunk, shard, False, False, False), sent)
        put_out(chunk).wait()
        return 0

    lax.fori_loop(0, n_chunks, finish, 0)


def pick_kernel(seg_count, n_chunks, spots, parts_ref, signs_ref, out_ref, table):
    stretch = parts_ref.shape[0] // n_chunks

    def join(at, _):
        base = pl.multiple_of(at * 8, 8)
        spans = [pl.ds(base + chunk * stretch, 8) for chunk in range(n_chunks)]
        parts = butterflies([parts_ref[span, :] for span in spans])
        for span, part in zip(spans, parts):
            table[span, :] = part
        return 0

    lax.fori_loop(0, stretch // 8, join, 0, unroll=2)

    lane = lax.broadcasted_iota(jnp.int32, (8, LANES), 1)
    chains = 4

    def pick(group, _):
        found = [jnp.zeros((8, LANES), jnp.float32)] * chains
        for at in range(LANES):
            spot = spots[group * LANES + at]
            values = table[pl.ds(lax.shift_right_logical(spot, 7), 8), :]
            values = pltpu.roll(values, spot & (LANES - 1), 1)
            found[at % chains] = jnp.where(lane == at, values, found[at % chains])
        both = (found[0] + found[1]) + (found[2] + found[3])
        out_ref[group] = both[:seg_count] * signs_ref[pl.ds(group, 1), :]
        return 0

    lax.fori_loop(0, out_ref.shape[0], pick, 0)


def local_sketch(acts, cots, bits, lengths, spots, signs, n_wide, n_narrow):
    tokens = acts.shape[0] * n_narrow
    rows, cols = bits.shape
    seg_count = lengths.shape[0]
    groups = signs.shape[0]
    cross = 2
    row_block, col_block = min(rows, 256), min(cols, 256)
    n_chunks = cols // col_block
    windows = []
    for seg in range(seg_count):
        low = max(0, tokens - (seg_count - seg) * MOST) // 256 * 256
        high = min(tokens, -(-(seg + 1) * MOST // 256) * 256)
        windows.append((low, high))
    ends = jnp.cumsum(lengths)
    bounds = jnp.stack([ends - lengths, ends]).astype(jnp.int32)
    gains = lax.rsqrt(lengths.astype(jnp.float32))
    anywhere = pl.BlockSpec(memory_space=pl.ANY)
    scalars = pl.BlockSpec(memory_space=pltpu.SMEM)
    vectors = pl.BlockSpec(memory_space=pltpu.VMEM)
    table = rows * cols // LANES * seg_count
    parts = pl.pallas_call(
        functools.partial(sketch_kernel, n_wide, n_narrow, cross, tuple(windows), n_chunks),
        out_shape=jax.ShapeDtypeStruct((table, LANES), jnp.float32),
        in_specs=[scalars] * 2 + [anywhere] * 3 + [vectors] * 2,
        out_specs=anywhere,
        scratch_shapes=[
            pltpu.VMEM((tokens, rows), acts.dtype),
            pltpu.VMEM((rows, cols), bits.dtype),
            pltpu.VMEM((rows, sum(high - low for low, high in windows)), jnp.bfloat16),
            pltpu.VMEM((table, LANES), jnp.float32),
            pltpu.VMEM((n_chunks, cots.shape[0] * n_wide, col_block), cots.dtype),
            pltpu.SemaphoreType.DMA((2 + 2 * n_chunks,)),
            pltpu.SemaphoreType.DMA((n_narrow,)),
            pltpu.SemaphoreType.DMA((n_narrow,)),
            pltpu.SemaphoreType.DMA((2 + cross, n_chunks, n_wide)),
            pltpu.SemaphoreType.DMA((n_chunks, n_wide)),
        ],
        compiler_params=pltpu.CompilerParams(
            collective_id=0, has_side_effects=True, vmem_limit_bytes=62 * 1024 * 1024
        ),
        name="local_sketch",
    )(bounds, gains, acts, cots, bits, sylvester(row_block), sylvester(col_block))
    return pl.pallas_call(
        functools.partial(pick_kernel, seg_count, n_chunks),
        out_shape=jax.ShapeDtypeStruct((groups, seg_count, LANES), jnp.float32),
        in_specs=[scalars, vectors, vectors],
        out_specs=vectors,
        scratch_shapes=[pltpu.VMEM((table + 8, LANES), jnp.float32)],
        compiler_params=pltpu.CompilerParams(vmem_limit_bytes=62 * 1024 * 1024),
        name="pick",
    )(spots, parts, signs)


def add_up_kernel(n_wide, n_narrow, shares, out, held, send_sem, recv_sem):
    count = n_wide * n_narrow
    me = lax.axis_index("wide") * n_narrow + lax.axis_index("narrow")
    barrier = pltpu.get_barrier_semaphore()

    def address(who):
        return {"wide": who // n_narrow, "narrow": lax.rem(who, n_narrow)}

    def greet(off, _):
        who = lax.rem(me + off, count)
        pl.semaphore_signal(barrier, inc=1, device_id=address(who), device_id_type=MESH)
        return 0

    lax.fori_loop(1, count, greet, 0)
    pl.semaphore_wait(barrier, count - 1)

    def copy_to(who, slot):
        return pltpu.make_async_remote_copy(
            src_ref=shares.at[who],
            dst_ref=held.at[slot],
            send_sem=send_sem.at[who],
            recv_sem=recv_sem.at[slot],
            device_id=address(who),
            device_id_type=MESH,
        )

    def send(off, _):
        copy_to(lax.rem(me + off, count), me).start()
        return 0

    lax.fori_loop(1, count, send, 0)
    out[...] = shares[me]

    def take(off, _):
        who = lax.rem(me + count - off, count)
        copy_to(who, who).wait_recv()
        out[...] += held[who]
        return 0

    lax.fori_loop(1, count, take, 0)

    def sent(off, _):
        copy_to(lax.rem(me + off, count), me).wait_send()
        return 0

    lax.fori_loop(1, count, sent, 0)


def add_up(shares, n_wide, n_narrow):
    count = n_wide * n_narrow
    in_vmem = pl.BlockSpec(memory_space=pltpu.VMEM)
    return pl.pallas_call(
        functools.partial(add_up_kernel, n_wide, n_narrow),
        out_shape=jax.ShapeDtypeStruct(shares.shape[1:], shares.dtype),
        in_specs=[in_vmem],
        out_specs=in_vmem,
        scratch_shapes=[
            pltpu.VMEM(shares.shape, shares.dtype),
            pltpu.SemaphoreType.DMA((count,)),
            pltpu.SemaphoreType.DMA((count,)),
        ],
        compiler_params=pltpu.CompilerParams(collective_id=1, has_side_effects=True),
        name="add_up",
    )(shares)


def body(n_wide, n_narrow, activations, cotangent, sign_bits, seg_lengths, kept_index):
    rows, cols = sign_bits.shape
    seg_count = seg_lengths.shape[0]
    kept = kept_index.shape[0]
    count = n_wide * n_narrow
    scale = 1.0 / math.sqrt(rows * n_wide * cols * n_narrow)
    full_cols = cols * n_narrow
    row_of = kept_index // full_cols
    col_of = kept_index % full_cols
    common = lax.population_count((row_of // rows) & lax.axis_index("wide"))
    common = common + lax.population_count((col_of // cols) & lax.axis_index("narrow"))
    signs = (1 - 2 * (common & 1)).astype(jnp.float32) * scale
    col = col_of % cols
    row = ((col // LANES) * rows + row_of % rows) * seg_count
    lane = jnp.arange(kept, dtype=jnp.int32)
    spots = row * LANES + ((lane - col) & (LANES - 1))
    shares = local_sketch(
        activations, cotangent, sign_bits, seg_lengths, spots, signs.reshape(-1, LANES),
        n_wide, n_narrow,
    )
    each = kept // count
    if each % LANES:
        flat = shares.transpose(1, 0, 2).reshape(seg_count, kept)
        return lax.psum_scatter(flat, ("wide", "narrow"), scatter_dimension=1, tiled=True)
    mine = add_up(shares.reshape(count, -1, LANES), n_wide, n_narrow)
    mine = mine.reshape(each // LANES, seg_count, LANES)
    return mine.transpose(1, 0, 2).reshape(seg_count, each)


def solution(mesh):
    return jax.shard_map(
        functools.partial(body, mesh.shape["wide"], mesh.shape["narrow"]),
        mesh=mesh,
        in_specs=(P("narrow", "wide"), P("wide", "narrow"), P("wide", "narrow"), P(), P()),
        out_specs=P(None, ("wide", "narrow")),
        check_vma=False,
    )
```

```python
import functools
import math

import jax
import jax.numpy as jnp
import numpy as np
from jax import lax
from jax.experimental import pallas as pl
from jax.experimental.pallas import tpu as pltpu
from jax.sharding import PartitionSpec as P

LANES = 128
MOST = 1536
MESH = pl.DeviceIdType.MESH


def sylvester(extent):
    indices = np.arange(extent)
    common = indices[:, None] & indices[None, :]
    parity = np.zeros((extent, extent), np.int64)
    for bit_pos in range(extent.bit_length() - 1):
        parity += common >> bit_pos & 1
    return jnp.asarray(1 - 2 * (parity % 2), jnp.bfloat16)


def butterflies(parts):
    parts = list(parts)
    gap = 1
    while gap < len(parts):
        for low in range(len(parts)):
            if not low & gap:
                one, two = parts[low], parts[low | gap]
                parts[low], parts[low | gap] = one + two, one - two
        gap *= 2
    return parts


def halves(values):
    high = values.astype(jnp.bfloat16)
    low = (values - high.astype(jnp.float32)).astype(jnp.bfloat16)
    return high, low


def sketch_kernel(
    n_wide, n_narrow, cross, windows, n_chunks,
    bounds, gains, acts, cots, bits_in, left_ref, right_ref,
    out_ref, acts_all, bits_ref, flipped, table, bufs,
    local_sem, acts_send, acts_recv, cots_send, cots_recv,
):
    wide = lax.axis_index("wide")
    narrow = lax.axis_index("narrow")
    lines = n_wide // (2 * cross)
    core = lax.rem(wide, 2)
    side = lax.rem(wide // 2, cross)
    place = wide // (2 * cross)
    tok_acts = acts.shape[0]
    tok_cots = cots.shape[0]
    rows, cols = bits_in.shape
    row_block = left_ref.shape[0]
    col_block = right_ref.shape[0]
    row_groups = rows // row_block
    per_group = col_block // LANES
    seg_count = len(windows)
    stretch = per_group * rows * seg_count

    def index_of(at, across, on_core):
        return (at * cross + across) * 2 + on_core

    partner = index_of(place, side, 1 - core)
    up = index_of(lax.rem(place + 1, lines), side, core)
    down = index_of(lax.rem(place + lines - 1, lines), side, core)
    across = [lax.rem(side + off, cross) for off in range(1, cross)]
    has_up = place < lines - 1
    has_down = place > 0

    my_acts = pl.ds(narrow * tok_acts, tok_acts)
    my_cots = pl.ds(wide * tok_cots, tok_cots)

    def columns_of(chunk):
        return pl.ds(pl.multiple_of(chunk * col_block, col_block), col_block)

    def own_cots(chunk):
        return pltpu.make_async_copy(
            cots.at[:, columns_of(chunk)], bufs.at[chunk, my_cots, :], local_sem.at[2 + chunk]
        )

    def put_out(chunk):
        span = pl.ds(pl.multiple_of(chunk * stretch, 8), stretch)
        return pltpu.make_async_copy(
            table.at[span, :], out_ref.at[span, :], local_sem.at[2 + n_chunks + chunk]
        )

    own_acts = pltpu.make_async_copy(acts, acts_all.at[my_acts, :], local_sem.at[0])
    own_bits = pltpu.make_async_copy(bits_in, bits_ref, local_sem.at[1])
    for chunk in range(n_chunks):
        own_cots(chunk).start()
    own_acts.start()
    own_bits.start()

    barrier = pltpu.get_barrier_semaphore()

    def greet(**where):
        pl.semaphore_signal(barrier, inc=1, device_id=where, device_id_type=MESH)

    greet(wide=partner)
    for other in across:
        greet(wide=index_of(place, other, core))
    for off in range(1, n_narrow):
        greet(narrow=lax.rem(narrow + off, n_narrow))

    @pl.when(has_up)
    def _():
        greet(wide=up)

    @pl.when(has_down)
    def _():
        greet(wide=down)

    ends = jnp.where(has_up, 1, 0) + jnp.where(has_down, 1, 0)
    pl.semaphore_wait(barrier, 1 + (cross - 1) + (n_narrow - 1) + ends)

    def acts_copy(off):
        return pltpu.make_async_remote_copy(
            src_ref=acts,
            dst_ref=acts_all.at[my_acts, :],
            send_sem=acts_send.at[off],
            recv_sem=acts_recv.at[off],
            device_id={"narrow": lax.rem(narrow + off, n_narrow)},
            device_id_type=MESH,
        )

    def cots_copy(chunk, way, shard, to):
        place_of = bufs.at[chunk, pl.ds(shard * tok_cots, tok_cots), :]
        return pltpu.make_async_remote_copy(
            src_ref=place_of,
            dst_ref=place_of,
            send_sem=cots_send.at[way, chunk, shard],
            recv_sem=cots_recv.at[chunk, shard],
            device_id={"wide": to},
            device_id_type=MESH,
        )

    def outgoing(chunk, shard, climbs, drops, crosses):
        todo = []
        if climbs:
            todo.append((has_up, cots_copy(chunk, 0, shard, up)))
        if drops:
            todo.append((has_down, cots_copy(chunk, 1, shard, down)))
        if crosses:
            for at, other in enumerate(across):
                to = index_of(place, other, core)
                todo.append((None, cots_copy(chunk, 3 + at, shard, to)))
        todo.append((None, cots_copy(chunk, 2, shard, partner)))
        return todo

    def each(todo, act):
        for condition, copy in todo:
            if condition is None:
                act(copy)
            else:
                pl.when(condition)(functools.partial(act, copy))

    def start(copy):
        copy.start()

    def sent(copy):
        copy.wait_send()

    def arrived(chunk, shard):
        cots_copy(chunk, 2, shard, partner).wait_recv()

    def from_lines(chunk, step, act, wait):
        @pl.when(place - step >= 0)
        def _():
            shard = index_of(place - step, side, core)
            if wait:
                arrived(chunk, shard)
            each(outgoing(chunk, shard, True, False, True), act)

        @pl.when(place + step < lines)
        def _():
            shard = index_of(place + step, side, core)
            if wait:
                arrived(chunk, shard)
            each(outgoing(chunk, shard, False, True, True), act)

    def from_cross(chunk, step):
        for other in across:
            for sign in (1,) if step == 0 else (-1, 1):
                at = place + sign * step

                @pl.when((at >= 0) & (at < lines))
                def _():
                    shard = index_of(at, other, core)
                    arrived(chunk, shard)
                    each(outgoing(chunk, shard, False, False, False), start)

    def launch(chunk):
        own_cots(chunk).wait()
        each(outgoing(chunk, wide, True, True, True), start)

    def prepare():
        own_acts.wait()
        for off in range(1, n_narrow):
            acts_copy(off).wait()
        own_bits.wait()
        tile = 256
        offset = 0
        for seg, (low, high) in enumerate(windows):

            def one(at, _):
                begin = pl.multiple_of(low + at * tile, tile)
                values = acts_all[pl.ds(begin, tile), :].astype(jnp.float32)
                where_at = begin + lax.broadcasted_iota(jnp.int32, values.shape, 0)
                inside = (where_at >= bounds[0, seg]) & (where_at < bounds[1, seg])
                values = jnp.where(inside, values, 0.0)
                spot = pl.multiple_of(offset + at * tile, tile)
                flipped[:, pl.ds(spot, tile)] = values.T.astype(jnp.bfloat16)
                return 0

            lax.fori_loop(0, (high - low) // tile, one, 0)
            offset += high - low

    def compute(chunk):
        for at in range(lines):
            for over in range(cross):
                arrived(chunk, index_of(at, over, 1 - core))

        columns = columns_of(chunk)
        offset = 0
        for seg, (low, high) in enumerate(windows):
            grad = jnp.dot(
                flipped[:, offset : offset + high - low],
                bufs[chunk, low:high, :],
                preferred_element_type=jnp.float32,
            )
            offset += high - low
            sign = (1 - 2 * bits_ref[:, columns]).astype(jnp.float32)
            grad = grad * (sign * gains[seg])
            parts = [
                grad[group * row_block : (group + 1) * row_block]
                for group in range(row_groups)
            ]
            for group, part in enumerate(butterflies(parts)):
                upper, lower = halves(part)
                mixed = jnp.dot(
                    left_ref[...], upper, preferred_element_type=jnp.float32
                ) + jnp.dot(left_ref[...], lower, preferred_element_type=jnp.float32)
                upper, lower = halves(mixed)
                mixed = jnp.dot(
                    upper, right_ref[...], preferred_element_type=jnp.float32
                ) + jnp.dot(lower, right_ref[...], preferred_element_type=jnp.float32)
                for lane_block in range(per_group):
                    block = chunk * per_group + lane_block
                    base = (block * rows + group * row_block) * seg_count + seg
                    table[pl.ds(base, row_block, stride=seg_count), :] = mixed[
                        :, lane_block * LANES : (lane_block + 1) * LANES
                    ]
        put_out(chunk).start()

    launch(0)
    for off in range(1, n_narrow):
        acts_copy(off).start()

    def slot_work(slot, _):
        @pl.when(slot + 1 < n_chunks)
        def _():
            launch(slot + 1)

        for step in range(lines, 0, -1):
            chunk = slot + 1 - step

            @pl.when((chunk >= 0) & (chunk < n_chunks))
            def _():
                if step < lines:
                    from_lines(chunk, step, start, True)
                from_cross(chunk, step - 1)

        pl.when(slot == lines + 1)(prepare)

        @pl.when(slot >= lines + 1)
        def _():
            compute(slot - lines - 1)

        return 0

    lax.fori_loop(0, n_chunks + lines + 1, slot_work, 0)

    def finish(chunk, _):
        each(outgoing(chunk, wide, True, True, True), sent)
        for step in range(1, lines):
            from_lines(chunk, step, sent, False)
        for at in range(lines):
            for other in across:
                shard = index_of(at, other, core)
                each(outgoing(chunk, shard, False, False, False), sent)
        put_out(chunk).wait()
        return 0

    lax.fori_loop(0, n_chunks, finish, 0)


def pick_kernel(seg_count, n_chunks, spots, parts_ref, signs_ref, out_ref, table):
    stretch = parts_ref.shape[0] // n_chunks

    def join(at, _):
        base = pl.multiple_of(at * 8, 8)
        spans = [pl.ds(base + chunk * stretch, 8) for chunk in range(n_chunks)]
        parts = butterflies([parts_ref[span, :] for span in spans])
        for span, part in zip(spans, parts):
            table[span, :] = part
        return 0

    lax.fori_loop(0, stretch // 8, join, 0, unroll=2)

    lane = lax.broadcasted_iota(jnp.int32, (8, LANES), 1)
    chains = 4

    def pick(group, _):
        found = [jnp.zeros((8, LANES), jnp.float32)] * chains
        for at in range(LANES):
            spot = spots[group * LANES + at]
            values = table[pl.ds(lax.shift_right_logical(spot, 7), 8), :]
            values = pltpu.roll(values, spot & (LANES - 1), 1)
            found[at % chains] = jnp.where(lane == at, values, found[at % chains])
        both = (found[0] + found[1]) + (found[2] + found[3])
        out_ref[group] = both[:seg_count] * signs_ref[pl.ds(group, 1), :]
        return 0

    lax.fori_loop(0, out_ref.shape[0], pick, 0)


def local_sketch(acts, cots, bits, lengths, spots, signs, n_wide, n_narrow):
    tokens = acts.shape[0] * n_narrow
    rows, cols = bits.shape
    seg_count = lengths.shape[0]
    groups = signs.shape[0]
    cross = 2
    row_block, col_block = min(rows, 256), min(cols, 256)
    n_chunks = cols // col_block
    windows = []
    for seg in range(seg_count):
        low = max(0, tokens - (seg_count - seg) * MOST) // 256 * 256
        high = min(tokens, -(-(seg + 1) * MOST // 256) * 256)
        windows.append((low, high))
    ends = jnp.cumsum(lengths)
    bounds = jnp.stack([ends - lengths, ends]).astype(jnp.int32)
    gains = lax.rsqrt(lengths.astype(jnp.float32))
    anywhere = pl.BlockSpec(memory_space=pl.ANY)
    scalars = pl.BlockSpec(memory_space=pltpu.SMEM)
    vectors = pl.BlockSpec(memory_space=pltpu.VMEM)
    table = rows * cols // LANES * seg_count
    parts = pl.pallas_call(
        functools.partial(sketch_kernel, n_wide, n_narrow, cross, tuple(windows), n_chunks),
        out_shape=jax.ShapeDtypeStruct((table, LANES), jnp.float32),
        in_specs=[scalars] * 2 + [anywhere] * 3 + [vectors] * 2,
        out_specs=anywhere,
        scratch_shapes=[
            pltpu.VMEM((tokens, rows), acts.dtype),
            pltpu.VMEM((rows, cols), bits.dtype),
            pltpu.VMEM((rows, sum(high - low for low, high in windows)), jnp.bfloat16),
            pltpu.VMEM((table, LANES), jnp.float32),
            pltpu.VMEM((n_chunks, cots.shape[0] * n_wide, col_block), cots.dtype),
            pltpu.SemaphoreType.DMA((2 + 2 * n_chunks,)),
            pltpu.SemaphoreType.DMA((n_narrow,)),
            pltpu.SemaphoreType.DMA((n_narrow,)),
            pltpu.SemaphoreType.DMA((2 + cross, n_chunks, n_wide)),
            pltpu.SemaphoreType.DMA((n_chunks, n_wide)),
        ],
        compiler_params=pltpu.CompilerParams(
            collective_id=0, has_side_effects=True, vmem_limit_bytes=62 * 1024 * 1024
        ),
        name="local_sketch",
    )(bounds, gains, acts, cots, bits, sylvester(row_block), sylvester(col_block))
    return pl.pallas_call(
        functools.partial(pick_kernel, seg_count, n_chunks),
        out_shape=jax.ShapeDtypeStruct((groups, seg_count, LANES), jnp.float32),
        in_specs=[scalars, vectors, vectors],
        out_specs=vectors,
        scratch_shapes=[pltpu.VMEM((table + 8, LANES), jnp.float32)],
        compiler_params=pltpu.CompilerParams(vmem_limit_bytes=62 * 1024 * 1024),
        name="pick",
    )(spots, parts, signs)


def add_up_kernel(n_wide, n_narrow, shares, out, held, send_sem, recv_sem):
    count = n_wide * n_narrow
    me = lax.axis_index("wide") * n_narrow + lax.axis_index("narrow")
    barrier = pltpu.get_barrier_semaphore()

    def address(who):
        return {"wide": who // n_narrow, "narrow": lax.rem(who, n_narrow)}

    def greet(off, _):
        who = lax.rem(me + off, count)
        pl.semaphore_signal(barrier, inc=1, device_id=address(who), device_id_type=MESH)
        return 0

    lax.fori_loop(1, count, greet, 0)
    pl.semaphore_wait(barrier, count - 1)

    def copy_to(who, slot):
        return pltpu.make_async_remote_copy(
            src_ref=shares.at[who],
            dst_ref=held.at[slot],
            send_sem=send_sem.at[who],
            recv_sem=recv_sem.at[slot],
            device_id=address(who),
            device_id_type=MESH,
        )

    def send(off, _):
        copy_to(lax.rem(me + off, count), me).start()
        return 0

    lax.fori_loop(1, count, send, 0)
    out[...] = shares[me]

    def take(off, _):
        who = lax.rem(me + count - off, count)
        copy_to(who, who).wait_recv()
        out[...] += held[who]
        return 0

    lax.fori_loop(1, count, take, 0)

    def sent(off, _):
        copy_to(lax.rem(me + off, count), me).wait_send()
        return 0

    lax.fori_loop(1, count, sent, 0)


def add_up(shares, n_wide, n_narrow):
    count = n_wide * n_narrow
    in_vmem = pl.BlockSpec(memory_space=pltpu.VMEM)
    return pl.pallas_call(
        functools.partial(add_up_kernel, n_wide, n_narrow),
        out_shape=jax.ShapeDtypeStruct(shares.shape[1:], shares.dtype),
        in_specs=[in_vmem],
        out_specs=in_vmem,
        scratch_shapes=[
            pltpu.VMEM(shares.shape, shares.dtype),
            pltpu.SemaphoreType.DMA((count,)),
            pltpu.SemaphoreType.DMA((count,)),
        ],
        compiler_params=pltpu.CompilerParams(collective_id=1, has_side_effects=True),
        name="add_up",
    )(shares)


def body(n_wide, n_narrow, activations, cotangent, sign_bits, seg_lengths, kept_index):
    rows, cols = sign_bits.shape
    seg_count = seg_lengths.shape[0]
    kept = kept_index.shape[0]
    count = n_wide * n_narrow
    scale = 1.0 / math.sqrt(rows * n_wide * cols * n_narrow)
    full_cols = cols * n_narrow
    row_of = kept_index // full_cols
    col_of = kept_index % full_cols
    common = lax.population_count((row_of // rows) & lax.axis_index("wide"))
    common = common + lax.population_count((col_of // cols) & lax.axis_index("narrow"))
    signs = (1 - 2 * (common & 1)).astype(jnp.float32) * scale
    col = col_of % cols
    row = ((col // LANES) * rows + row_of % rows) * seg_count
    lane = jnp.arange(kept, dtype=jnp.int32)
    spots = row * LANES + ((lane - col) & (LANES - 1))
    shares = local_sketch(
        activations, cotangent, sign_bits, seg_lengths, spots, signs.reshape(-1, LANES),
        n_wide, n_narrow,
    )
    each = kept // count
    if each % LANES:
        flat = shares.transpose(1, 0, 2).reshape(seg_count, kept)
        return lax.psum_scatter(flat, ("wide", "narrow"), scatter_dimension=1, tiled=True)
    mine = add_up(shares.reshape(count, -1, LANES), n_wide, n_narrow)
    mine = mine.reshape(each // LANES, seg_count, LANES)
    return mine.transpose(1, 0, 2).reshape(seg_count, each)


def solution(mesh):
    return jax.shard_map(
        functools.partial(body, mesh.shape["wide"], mesh.shape["narrow"]),
        mesh=mesh,
        in_specs=(P("narrow", "wide"), P("wide", "narrow"), P("wide", "narrow"), P(), P()),
        out_specs=P(None, ("wide", "narrow")),
        check_vma=False,
    )
```
